512 devices in a mesh: space: 32 (over x, y, core), vel: 16 (over z).
Axes of the slice: x: 4, y: 4, z: 16, core: 2. Of those that a mesh axis runs over, the one named last changes fastest.
Arguments:
- distribution: float32 [4096, 32768], P('vel', 'space'), may hold values from -48 to 48
- kernel: bfloat16 [4096, 4096], P('vel'), may hold values from -0.046875 to 0.046875
- frequency: float32 [4096], P('vel'), may hold values from 0.05 to 0.5
- accommodation: float32 [8], replicated, may hold values from 0.2 to 0.95
- wall_class: int32 [2, 1024], P(None, 'space'), may hold values from 0 to 7
Outputs:
- updated: float32 [4096, 32768], P('vel', 'space')
The draws below stay inside these ranges and needn't reach their ends.
All inputs are finite; a program needn't handle non-finite values.
Results may differ from the reference program's by a relative error of at most 0.0018.
Values may be sent and summed in bfloat16 or wider, within the bound.
No kernel may reach another device: no remote copies, remote signals or barrier semaphores. Data moves between devices by JAX's collectives and lax.ppermute only.
A program may use at most 64 MiB of HBM per device.

```python
import math
import jax
import jax.numpy as jnp

NV1 = 16
V = 4096
NY = 32
NX = 1024
NCLASS = 8


def draw_distribution(key, part):
    key_rows, key_cols, key_noise = jax.random.split(key, 3)
    row_scale = jnp.exp(jax.random.uniform(key_rows, (V, 1), jnp.float32, math.log(0.3), math.log(3.0)))
    col_scale = jnp.exp(jax.random.uniform(key_cols, (1, NX * NY), jnp.float32, math.log(0.4), math.log(4.0)))
    noise = jax.random.truncated_normal(key_noise, -4.0, 4.0, (V, NX * NY), jnp.float32)
    return row_scale * noise * col_scale


def set_ends(drawn, own_key, low, largest):
    shape = drawn.shape
    spot = [jax.random.randint(jax.random.fold_in(own_key, axis), (), 0, shape[axis]) for axis in range(len(shape))]
    drawn = drawn.at[tuple(spot)].set(low)
    longest = shape.index(max(shape))
    spot[longest] = (spot[longest] + 1) % shape[longest]
    return drawn.at[tuple(spot)].set(largest)


def shard_levels(own_key, dims, cuts, low, high):
    loudness, own = 1.0, jax.random.fold_in(own_key, 6)
    for axis_at, blocks in cuts:
        draws = jnp.exp(jax.random.uniform(jax.random.fold_in(own, axis_at), (blocks,), jnp.float32, low / len(cuts), high / len(cuts)))
        loudness = loudness * jnp.repeat(draws, dims[axis_at] // blocks).reshape([-1 if axis == axis_at else 1 for axis in range(len(dims))])
    return loudness


def gaussian(stream_key, dims, scale, most, cuts=(), held_as=jnp.bfloat16):
    drawn = scale * jax.random.normal(stream_key, dims, jnp.float32)
    if cuts:
        drawn = drawn * shard_levels(stream_key, dims, cuts, -0.22, 0.18)
    return jnp.clip(drawn, -most, most).astype(held_as)


def setup_inputs(seed: int = 0) -> dict:
    key_list = jax.random.split(jax.random.key(seed), 6)
    return {
        "distribution": draw_distribution(jax.random.fold_in(key_list[5], 71), 0),
        "kernel": gaussian(key_list[1], (V, V), (4 * V) ** -0.5, 0.046875, ((0, 16),)),
        "frequency": jnp.clip(jnp.exp(math.log(0.5) - 2.3025851 * jax.random.uniform(key_list[2], (V,), jnp.float32) ** shard_levels(key_list[2], (V,), ((0, 16),), -0.2, 0.2)), 0.05, 0.5),
        "accommodation": jnp.clip(jax.random.uniform(key_list[3], (NCLASS,), jnp.float32, 0.2, 0.95), 0.2, 0.95),
        "wall_class": set_ends(jax.random.randint(key_list[4], (2, NX), 0, NCLASS), jax.random.fold_in(key_list[4], 1), 0, NCLASS - 1).astype(jnp.int32),
    }


courant_x = 0.05
courant_y = 0.15


def velocity_parts(vel_index):
    spacing = 9.6 / NV1
    middle = (NV1 - 1) / 2.0
    index_y = vel_index // (NV1 * NV1)
    index_x = (vel_index // NV1) % NV1
    index_z = vel_index % NV1
    vel_x = (index_x.astype(jnp.float32) - middle) * spacing
    vel_y = (index_y.astype(jnp.float32) - middle) * spacing
    vel_z = (index_z.astype(jnp.float32) - middle) * spacing
    return vel_x, vel_y, vel_z


def grid_constants():
    spacing = 9.6 / NV1
    middle = (NV1 - 1) / 2.0
    points = (jnp.arange(NV1, dtype=jnp.int32).astype(jnp.float32) - middle) * spacing
    weights = jnp.exp(-0.5 * points * points)
    zsum = jnp.sum(weights)
    outflow = jnp.sum(jnp.where(points > 0, points * weights, 0.0)) / zsum
    return zsum * zsum * zsum, outflow


def reference(distribution, kernel, frequency, accommodation, wall_class):
    vel_x, vel_y, vel_z = velocity_parts(jnp.arange(V, dtype=jnp.int32))
    normal_sum, outflow = grid_constants()
    maxwell = jnp.exp(-0.5 * (vel_x * vel_x + vel_y * vel_y + vel_z * vel_z)) / normal_sum
    field = distribution.reshape(V, NX, NY)
    lowered = distribution.astype(jnp.bfloat16)
    low_field = lowered.reshape(V, NX, NY)
    lower = low_field[:, :, 0].astype(jnp.float32)
    upper = low_field[:, :, NY - 1].astype(jnp.float32)
    down_weight = jnp.where(vel_y < 0, -vel_y, 0.0)
    up_weight = jnp.where(vel_y > 0, vel_y, 0.0)
    sigma_low = jnp.sum(down_weight[:, None] * lower, axis=0) / outflow
    sigma_up = jnp.sum(up_weight[:, None] * upper, axis=0) / outflow
    alpha = accommodation[wall_class]
    mirror_low = lower.reshape(NV1, NV1 * NV1, NX)[::-1].reshape(V, NX)
    mirror_up = upper.reshape(NV1, NV1 * NV1, NX)[::-1].reshape(V, NX)
    inflow_low = alpha[0][None, :] * sigma_low[None, :] * maxwell[:, None] + (1.0 - alpha[0])[None, :] * mirror_low
    inflow_up = alpha[1][None, :] * sigma_up[None, :] * maxwell[:, None] + (1.0 - alpha[1])[None, :] * mirror_up
    left = jnp.roll(field, 1, axis=1)
    right = jnp.roll(field, -1, axis=1)
    below = jnp.concatenate([inflow_low[:, :, None], field[:, :, :-1]], axis=2)
    above = jnp.concatenate([field[:, :, 1:], inflow_up[:, :, None]], axis=2)
    move_x = courant_x * (jnp.maximum(vel_x, 0.0)[:, None, None] * (field - left) + jnp.minimum(vel_x, 0.0)[:, None, None] * (right - field))
    move_y = courant_y * (jnp.maximum(vel_y, 0.0)[:, None, None] * (field - below) + jnp.minimum(vel_y, 0.0)[:, None, None] * (above - field))
    moved = (move_x + move_y).reshape(V, NX * NY)
    gain = jnp.dot(kernel, lowered, preferred_element_type=jnp.float32)
    return distribution - moved - frequency[:, None] * distribution + gain
```

```python
import functools

import jax
import jax.numpy as jnp
import numpy as np
from jax import lax
from jax.experimental import pallas as pl
from jax.experimental.pallas import tpu as pltpu
from jax.sharding import PartitionSpec as P

NV1 = 16
NY = 32
NCLASS = 8
SPACING = 9.6 / NV1
MIDDLE = (NV1 - 1) / 2.0
EXTRA = 16
ADD_AT = 4
CHAINS = (0, 2, 1)

courant_x = 0.05
courant_y = 0.15


POINTS = (np.arange(NV1) - MIDDLE) * SPACING
WEIGHTS = np.exp(-0.5 * POINTS * POINTS)
ZSUM = float(WEIGHTS.sum())
OUTFLOW = float((POINTS * WEIGHTS)[POINTS > 0].sum() / ZSUM)


def base_kernel(scal_ref, d_ref, halo_ref, head_ref, tail_ref, freq_ref, out_ref):
    rows, cells = d_ref.shape
    speed = scal_ref[0]
    upward = scal_ref[1]
    core = scal_ref[2]
    y_place = lax.broadcasted_iota(jnp.int32, (NV1, cells), 1) % NY
    lane = lax.broadcasted_iota(jnp.int32, (NV1, 128), 1)

    def halves(y_shift, y_edge):
        def chunk(positive, i, carry):
            here = pl.ds(pl.multiple_of(i * NV1, NV1), NV1)
            speed_x = courant_x * jnp.abs((i.astype(jnp.float32) - MIDDLE) * SPACING)
            g = d_ref[here, :]
            halo = halo_ref[here, :].astype(jnp.float32)
            if positive:
                outside = jnp.where(core == 0.0, halo, tail_ref[here, :].astype(jnp.float32))
                beside = pltpu.roll(g, NY, 1)
                tile = jnp.where(lane < NY, pltpu.roll(outside, NY, 1), beside[:, :128])
                beside = jnp.concatenate([tile, beside[:, 128:]], axis=1)
            else:
                outside = jnp.where(core == 0.0, head_ref[here, :].astype(jnp.float32), halo)
                beside = pltpu.roll(g, cells - NY, 1)
                tile = jnp.where(lane >= 128 - NY, pltpu.roll(outside, 128 - NY, 1), beside[:, cells - 128 :])
                beside = jnp.concatenate([beside[:, : cells - 128], tile], axis=1)
            over = jnp.where(y_place == y_edge, 0.0, pltpu.roll(g, y_shift, 1))
            out_ref[here, :] = g - (speed_x * (g - beside) + speed * (g - over)) - freq_ref[here, :] * g
            return carry

        lax.fori_loop(0, rows // NV1 // 2, functools.partial(chunk, False), 0)
        lax.fori_loop(rows // NV1 // 2, rows // NV1, functools.partial(chunk, True), 0)

    @pl.when(upward > 0.0)
    def _():
        halves(1, 0)

    @pl.when(upward <= 0.0)
    def _():
        halves(cells - 1, NY - 1)


def base_part(scal, distribution, halo, near, far, frequency):
    rows, cells = distribution.shape
    smem = pl.BlockSpec(memory_space=pltpu.SMEM)
    whole = pl.BlockSpec((rows, cells), lambda i: (0, 0))
    thin = pl.BlockSpec((rows, 128), lambda i: (0, 0))
    last = far.shape[1] // 128 - 1
    return pl.pallas_call(
        base_kernel,
        grid=(1,),
        out_shape=jax.ShapeDtypeStruct(distribution.shape, jnp.float32),
        in_specs=[smem, whole, thin, thin, pl.BlockSpec((rows, 128), lambda i: (0, last)), pl.BlockSpec((rows, 1), lambda i: (0, 0))],
        out_specs=whole,
        cost_estimate=pl.CostEstimate(flops=10_000_000, bytes_accessed=3_000_000, transcendentals=0),
    )(scal, distribution, halo, near, far, frequency)


def split_kernel(core_ref, d_ref, first_ref, last_ref, near_ref, far_ref, edge_ref):
    cells = d_ref.shape[1]
    low = d_ref[...].astype(jnp.bfloat16)
    first_ref[...] = low[:, : first_ref.shape[1]]
    last_ref[...] = low[:, first_ref.shape[1] :]
    near_ref[...] = low[:, : near_ref.shape[1]]
    far_ref[...] = low[:, near_ref.shape[1] :]

    @pl.when(core_ref[0] == 0)
    def _():
        edge_ref[...] = low[:, :128]

    @pl.when(core_ref[0] != 0)
    def _():
        edge_ref[...] = low[:, cells - 128 :]


def split_part(core, distribution, cut, mixed):
    rows, cells = distribution.shape
    widths = (cut, cells - cut, mixed, cells - mixed, 128)
    part = rows // 4
    return pl.pallas_call(
        split_kernel,
        grid=(4,),
        out_shape=[jax.ShapeDtypeStruct((rows, width), jnp.bfloat16) for width in widths],
        in_specs=[pl.BlockSpec(memory_space=pltpu.SMEM), pl.BlockSpec((part, cells), lambda i: (i, 0))],
        out_specs=[pl.BlockSpec((part, width), lambda i: (i, 0)) for width in widths],
        cost_estimate=pl.CostEstimate(flops=1_000_000, bytes_accessed=3_000_000, transcendentals=0),
    )(core, distribution)


def per_device(distribution, kernel, frequency, accommodation, wall_class):
    rows, cells = distribution.shape
    ranks = lax.axis_size("vel")
    places = lax.axis_size("space")
    rank = lax.axis_index("vel")
    core = lax.axis_index("space") & 1
    f32, bf16 = jnp.float32, jnp.bfloat16
    half = ranks // 2

    ring = [(s * ranks + v, s * ranks + (v + (1 if s % 2 == 0 else -1)) % ranks) for s in range(places) for v in range(ranks)]
    pair = [(s, s ^ 1) for s in range(places)]
    beyond = [(s, (s + (1 if s % 2 else -1)) % places) for s in range(places)]

    def hop(values):
        return lax.ppermute(values, ("space", "vel"), ring)

    def swap(values):
        return lax.ppermute(values, "space", pair)

    cut, mixed = 5 * cells // 8, cells // 4
    own = cells - cut
    first, last, near, far, edge = split_part(core[None], distribution, cut, mixed)
    far = swap(far)
    near = swap(near)
    held = [first, jnp.concatenate([last, near], axis=1), far]

    lower_half = rank < half
    at_wall = lax.broadcasted_iota(jnp.int32, (1, cells), 1) % NY == jnp.where(lower_half, NY - 1, 0)
    classes = jnp.where(lower_half, wall_class[1], wall_class[0])
    class_ids = lax.iota(jnp.int32, NCLASS)
    alpha = jnp.sum(jnp.where(classes[:, None] == class_ids[None, :], accommodation[None, :], 0.0), axis=1)
    alpha = jnp.repeat(alpha, NY)[None, :]
    vel_y = (rank.astype(f32) - MIDDLE) * SPACING
    speed = courant_y * jnp.abs(vel_y)
    keep = jnp.where(at_wall, speed * (1.0 - alpha), 0.0)
    share = jnp.where(at_wall, alpha * (0.5 * SPACING / OUTFLOW), 0.0)
    their_keep = swap(keep)
    keeps = [keep[:, :cut], jnp.concatenate([keep[:, cut:], their_keep[:, :mixed]], axis=1), their_keep[:, mixed:]]

    block = lax.broadcasted_iota(jnp.int32, (EXTRA, kernel.shape[1]), 1) // rows
    outgoing = (block < half) != lower_half
    weight = jnp.where(outgoing, jnp.abs(2 * block - (NV1 - 1)), 0).astype(bf16)
    wide = jnp.concatenate([kernel, weight], axis=0)

    def origin(step):
        return (rank + jnp.where(core == 0, -step, step)) & (ranks - 1)

    def part(step, values):
        return jnp.dot(
            lax.dynamic_slice_in_dim(wide, origin(step) * rows, rows, axis=1), values, preferred_element_type=f32
        )

    halo = lax.ppermute(edge, "space", beyond)
    scal = jnp.stack([speed, jnp.where(vel_y > 0.0, 1.0, -1.0), core.astype(f32)])
    base = base_part(scal, distribution, halo, near, far, frequency[:, None])

    sums = [part(0, first), jnp.pad(part(0, last), ((0, 0), (0, mixed))), None]
    for step in range(1, half):
        for j in CHAINS:
            held[j] = hop(held[j])
            if step == ADD_AT and j == 0:
                held[0], sums[0], base = lax.optimization_barrier((held[0], sums[0], base))
            elif step > 1 and step < half - 1:
                held[j], sums[j] = lax.optimization_barrier((held[j], sums[j]))
        for j in CHAINS:
            mirrored = jnp.where(origin(step) == ranks - 1 - rank, keeps[j], 0.0)
            given = part(step, held[j])
            if step % 2 == 1:
                given = given + jnp.pad(mirrored * held[j].astype(f32), ((0, EXTRA), (0, 0)))
            if step == ADD_AT and j == 0:
                given = given + jnp.pad(base[:, :cut], ((0, EXTRA), (0, 0)))
            if step == ADD_AT and j == 1:
                given = given + jnp.pad(base[:, cut:], ((0, EXTRA), (0, mixed)))
            sums[j] = given if sums[j] is None else sums[j] + given
    final = jnp.concatenate([hop(held[0]), hop(held[1][:, :own])], axis=1)
    given = swap(jnp.concatenate([sums[1][:, own:], sums[2]], axis=1))

    index = lax.iota(jnp.int32, rows)
    vel_x = ((index // NV1 % NV1).astype(f32) - MIDDLE) * SPACING
    vel_z = ((index % NV1).astype(f32) - MIDDLE) * SPACING
    maxwell = jnp.exp(-0.5 * (vel_x * vel_x + vel_y * vel_y + vel_z * vel_z)) * (speed / ZSUM**3)

    mine = jnp.concatenate([sums[0], sums[1][:, :own]], axis=1)
    total = mine + given + part(half, final)
    return total[:rows] + maxwell[:, None] * (total[rows : rows + 1] * share)


def solution(mesh):
    placed = (P("vel", "space"), P("vel", None), P("vel"), P(), P(None, "space"))
    return jax.shard_map(per_device, mesh=mesh, in_specs=placed, out_specs=P("vel", "space"), check_vma=False)
```

```python
import functools

import jax
import jax.numpy as jnp
import numpy as np
from jax import lax
from jax.experimental import pallas as pl
from jax.experimental.pallas import tpu as pltpu
from jax.sharding import PartitionSpec as P

NV1 = 16
NY = 32
NCLASS = 8
SPACING = 9.6 / NV1
MIDDLE = (NV1 - 1) / 2.0
EXTRA = 16
ADD_AT = 6

courant_x = 0.05
courant_y = 0.15


POINTS = (np.arange(NV1) - MIDDLE) * SPACING
WEIGHTS = np.exp(-0.5 * POINTS * POINTS)
ZSUM = float(WEIGHTS.sum())
OUTFLOW = float((POINTS * WEIGHTS)[POINTS > 0].sum() / ZSUM)


def base_kernel(positive, scal_ref, d_ref, halo_ref, pair_ref, freq_ref, out_ref):
    rows, cells = d_ref.shape
    speed = scal_ref[0]
    upward = scal_ref[1]
    core = scal_ref[2]
    y_place = lax.broadcasted_iota(jnp.int32, (NV1, cells), 1) % NY
    lane = lax.broadcasted_iota(jnp.int32, (NV1, 128), 1)
    from_pair = core if positive else 1.0 - core

    def loop(y_shift, y_edge):
        def chunk(i, carry):
            here = pl.ds(pl.multiple_of(i * NV1, NV1), NV1)
            index_x = i + (rows // NV1 if positive else 0)
            speed_x = courant_x * jnp.abs((index_x.astype(jnp.float32) - MIDDLE) * SPACING)
            g = d_ref[here, :]
            outside = jnp.where(from_pair == 1.0, pair_ref[here, :], halo_ref[here, :]).astype(jnp.float32)
            if positive:
                beside = pltpu.roll(g, NY, 1)
                tile = jnp.where(lane < NY, pltpu.roll(outside, NY, 1), beside[:, :128])
                beside = jnp.concatenate([tile, beside[:, 128:]], axis=1)
            else:
                beside = pltpu.roll(g, cells - NY, 1)
                tile = jnp.where(lane >= 128 - NY, pltpu.roll(outside, 128 - NY, 1), beside[:, cells - 128 :])
                beside = jnp.concatenate([beside[:, : cells - 128], tile], axis=1)
            over = jnp.where(y_place == y_edge, 0.0, pltpu.roll(g, y_shift, 1))
            out_ref[here, :] = g - (speed_x * (g - beside) + speed * (g - over)) - freq_ref[here, :] * g
            return carry

        lax.fori_loop(0, rows // NV1, chunk, 0)

    @pl.when(upward > 0.0)
    def _():
        loop(1, 0)

    @pl.when(upward <= 0.0)
    def _():
        loop(cells - 1, NY - 1)


def base_part(positive, scal, distribution, halo, pair_edge, frequency):
    rows, cells = distribution.shape
    part = rows // 2
    smem = pl.BlockSpec(memory_space=pltpu.SMEM)
    at = lambda i: (int(positive), 0)
    thin = pl.BlockSpec((part, 128), at)
    return pl.pallas_call(
        functools.partial(base_kernel, positive),
        grid=(1,),
        out_shape=jax.ShapeDtypeStruct((part, cells), jnp.float32),
        in_specs=[smem, pl.BlockSpec((part, cells), at), thin, thin, pl.BlockSpec((part, 1), at)],
        out_specs=pl.BlockSpec((part, cells), lambda i: (0, 0)),
        compiler_params=pltpu.CompilerParams(vmem_limit_bytes=6 << 20),
        cost_estimate=pl.CostEstimate(flops=5_000_000, bytes_accessed=1_500_000, transcendentals=0),
    )(scal, distribution, halo, pair_edge, frequency)


def per_device(distribution, kernel, frequency, accommodation, wall_class):
    rows, cells = distribution.shape
    ranks = lax.axis_size("vel")
    places = lax.axis_size("space")
    rank = lax.axis_index("vel")
    core = lax.axis_index("space") & 1
    f32, bf16 = jnp.float32, jnp.bfloat16
    half = ranks // 2

    ring = [(s * ranks + v, s * ranks + (v + (1 if s % 2 == 0 else -1)) % ranks) for s in range(places) for v in range(ranks)]
    pair = [(s, s ^ 1) for s in range(places)]
    beyond = [(s, (s + (1 if s % 2 else -1)) % places) for s in range(places)]

    cross = [
        (s * ranks + v, (s ^ 1) * ranks + (v + (-1 if s % 2 == 0 else 1)) % ranks) for s in range(places) for v in range(ranks)
    ]

    def hop(values, way=ring):
        return lax.ppermute(values, ("space", "vel"), way)

    def swap(values, way=pair):
        return lax.ppermute(values, "space", way)

    low = distribution.astype(bf16)
    held = [hop(low), hop(low, cross)]

    lower_half = rank < half
    at_wall = lax.broadcasted_iota(jnp.int32, (1, cells), 1) % NY == jnp.where(lower_half, NY - 1, 0)
    classes = jnp.where(lower_half, wall_class[1], wall_class[0])
    class_ids = lax.iota(jnp.int32, NCLASS)
    alpha = jnp.sum(jnp.where(classes[:, None] == class_ids[None, :], accommodation[None, :], 0.0), axis=1)
    alpha = jnp.repeat(alpha, NY)[None, :]
    vel_y = (rank.astype(f32) - MIDDLE) * SPACING
    speed = courant_y * jnp.abs(vel_y)
    keep = jnp.where(at_wall, speed * (1.0 - alpha), 0.0)
    share = jnp.where(at_wall, alpha * (0.5 * SPACING / OUTFLOW), 0.0)
    their_keep = swap(keep)
    keeps = [keep, their_keep]

    block = lax.broadcasted_iota(jnp.int32, (EXTRA, kernel.shape[1]), 1) // rows
    outgoing = (block < half) != lower_half
    weight = jnp.where(outgoing, jnp.abs(2 * block - (NV1 - 1)), 0).astype(bf16)
    wide = jnp.concatenate([kernel, weight], axis=0)

    def origin(step):
        return (rank + jnp.where(core == 0, -step, step)) & (ranks - 1)

    def part(step, values):
        return jnp.dot(
            lax.dynamic_slice_in_dim(wide, origin(step) * rows, rows, axis=1), values, preferred_element_type=f32
        )

    head, tail = low[:, :128], low[:, cells - 128 :]
    outer, inner = jnp.where(core == 0, head, tail), jnp.where(core == 0, tail, head)
    halo = swap(outer, beyond)
    pair_edge = swap(inner)
    scal = jnp.stack([speed, jnp.where(vel_y > 0.0, 1.0, -1.0), core.astype(f32)])
    column = frequency[:, None]
    base = []
    for positive in (False, True):
        base.append(base_part(positive, scal, distribution, halo, pair_edge, column))

    sums = [part(0, low), None]
    due = [[], []]
    for step in range(1, half):
        for j in (0, 1):
            if step > 1:
                held[j] = hop(held[j])
                if step == ADD_AT and j == 0:
                    held[0], sums[0], base = lax.optimization_barrier((held[0], sums[0], base))
                elif step < half - 1:
                    held[j], sums[j] = lax.optimization_barrier((held[j], sums[j]))
        for j in (0, 1):
            mirrored = (jnp.where(origin(step) == ranks - 1 - rank, keeps[j], 0.0), held[j])
            if step % 2 == 1 and (step > 1 or j == 0):
                due[j].append(mirrored)
            given = part(step, held[j])
            for row, values in due[j]:
                given = given + jnp.pad(row * values.astype(f32), ((0, EXTRA), (0, 0)))
            due[j] = []
            if step == ADD_AT and j == 0:
                for i, piece in enumerate(base):
                    below = rows + EXTRA - (i + 1) * (rows // 2)
                    given = given + jnp.pad(piece, ((i * (rows // 2), below), (0, 0)))
            sums[j] = given if sums[j] is None else sums[j] + given
            if step == 1 and j == 1:
                due[j].append(mirrored)
    final = hop(held[0])
    given = swap(sums[1])

    index = lax.iota(jnp.int32, rows)
    vel_x = ((index // NV1 % NV1).astype(f32) - MIDDLE) * SPACING
    vel_z = ((index % NV1).astype(f32) - MIDDLE) * SPACING
    maxwell = jnp.exp(-0.5 * (vel_x * vel_x + vel_y * vel_y + vel_z * vel_z)) * (speed / ZSUM**3)

    total = sums[0] + given + part(half, final)
    return total[:rows] + maxwell[:, None] * (total[rows : rows + 1] * share)


def solution(mesh):
    placed = (P("vel", "space"), P("vel", None), P("vel"), P(), P(None, "space"))
    return jax.shard_map(per_device, mesh=mesh, in_specs=placed, out_specs=P("vel", "space"), check_vma=False)
```

```python
import functools

import jax
import jax.numpy as jnp
import numpy as np
from jax import lax
from jax.experimental import pallas as pl
from jax.experimental.pallas import tpu as pltpu
from jax.sharding import PartitionSpec as P

NV1 = 16
NY = 32
SPACING = 9.6 / NV1
MIDDLE = (NV1 - 1) / 2.0
EXTRA = 16
ADD_AT = 6

courant_x = 0.05
courant_y = 0.15


POINTS = (np.arange(NV1) - MIDDLE) * SPACING
WEIGHTS = np.exp(-0.5 * POINTS * POINTS)
ZSUM = float(WEIGHTS.sum())
OUTFLOW = float((POINTS * WEIGHTS)[POINTS > 0].sum() / ZSUM)


def speed_y(rank):
    return courant_y * jnp.abs((rank.astype(jnp.float32) - MIDDLE) * SPACING)


def wall_kernel(info_ref, class_ref, alpha_ref, keep_ref, share_ref):
    cells = keep_ref.shape[1]
    rank = info_ref[0]
    side = jnp.where(rank < NV1 // 2, 1, 0)
    lane = lax.broadcasted_iota(jnp.int32, (1, cells), 1)
    alpha = jnp.zeros((1, cells), jnp.float32)
    for x in range(cells // NY):
        alpha = jnp.where(lane // NY == x, alpha_ref[class_ref[side, x]], alpha)
    at_wall = lane % NY == jnp.where(rank < NV1 // 2, NY - 1, 0)
    keep_ref[...] = jnp.where(at_wall, speed_y(rank) * (1.0 - alpha), 0.0)
    share_ref[...] = jnp.where(at_wall, alpha * (0.5 * SPACING / OUTFLOW), 0.0)


def wall_part(info, wall_class, accommodation, cells):
    smem = pl.BlockSpec(memory_space=pltpu.SMEM)
    vmem = pl.BlockSpec(memory_space=pltpu.VMEM)
    return pl.pallas_call(
        wall_kernel,
        out_shape=[jax.ShapeDtypeStruct((1, cells), jnp.float32)] * 2,
        in_specs=[smem, smem, smem],
        out_specs=[vmem, vmem],
        compiler_params=pltpu.CompilerParams(vmem_limit_bytes=1 << 20),
        cost_estimate=pl.CostEstimate(flops=100_000, bytes_accessed=10_000, transcendentals=0),
    )(info, wall_class, accommodation)


def last_kernel(info_ref, kernel_ref, acc_ref, far_ref, share_ref, out_ref):
    rows = out_ref.shape[0]
    rank = info_ref[0]
    far = (rank + NV1 // 2) & (NV1 - 1)
    values = far_ref[...]
    weight = jnp.abs(2 * far - (NV1 - 1)).astype(jnp.float32)
    flux = acc_ref[rows : rows + 1, :] + weight * jnp.sum(values.astype(jnp.float32), axis=0, keepdims=True)
    gain = jnp.dot(kernel_ref[...], values, preferred_element_type=jnp.float32)
    index = lax.broadcasted_iota(jnp.int32, (rows, 1), 0)
    vel_x = ((index // NV1).astype(jnp.float32) - MIDDLE) * SPACING
    vel_z = ((index % NV1).astype(jnp.float32) - MIDDLE) * SPACING
    vel_y = (rank.astype(jnp.float32) - MIDDLE) * SPACING
    maxwell = jnp.exp(-0.5 * (vel_x * vel_x + vel_y * vel_y + vel_z * vel_z)) * (speed_y(rank) / ZSUM**3)
    out_ref[...] = acc_ref[:rows, :] + gain + maxwell * (flux * share_ref[...])


def last_part(info, kernel, acc, far, share):
    rows, cells = far.shape
    width = cells // 4
    far_of = lambda info: (info[0] + NV1 // 2) & (NV1 - 1)
    return pl.pallas_call(
        last_kernel,
        grid_spec=pltpu.PrefetchScalarGridSpec(
            num_scalar_prefetch=1,
            grid=(4,),
            in_specs=[
                pl.BlockSpec((rows, rows), lambda i, info: (0, far_of(info))),
                pl.BlockSpec((acc.shape[0], width), lambda i, info: (0, i)),
                pl.BlockSpec((rows, width), lambda i, info: (0, i)),
                pl.BlockSpec((1, width), lambda i, info: (0, i)),
            ],
            out_specs=pl.BlockSpec((rows, width), lambda i, info: (0, i)),
        ),
        out_shape=jax.ShapeDtypeStruct((rows, cells), jnp.float32),
        compiler_params=pltpu.CompilerParams(vmem_limit_bytes=6 << 20),
        cost_estimate=pl.CostEstimate(flops=2 * rows * rows * cells, bytes_accessed=3_000_000, transcendentals=0),
    )(info, kernel, acc, far, share)


def base_kernel(positive, info_ref, d_ref, halo_ref, pair_ref, freq_ref, out_ref):
    rows, cells = d_ref.shape
    rank = info_ref[0]
    core = info_ref[1]
    speed = speed_y(rank)
    sub = lax.broadcasted_iota(jnp.int32, (NV1, rows), 0)
    freq_lane = lax.broadcasted_iota(jnp.int32, (NV1, rows), 1)
    y_place = lax.broadcasted_iota(jnp.int32, (NV1, cells), 1) % NY
    lane = lax.broadcasted_iota(jnp.int32, (NV1, 128), 1)
    from_pair = core if positive else 1 - core

    def loop(y_shift, y_edge):
        def chunk(i, carry):
            here = pl.ds(pl.multiple_of(i * NV1, NV1), NV1)
            index_x = i + (rows // NV1 if positive else 0)
            speed_x = courant_x * jnp.abs((index_x.astype(jnp.float32) - MIDDLE) * SPACING)
            g = d_ref[here, :]
            outside = jnp.where(from_pair == 1, pair_ref[here, :], halo_ref[here, :]).astype(jnp.float32)
            if positive:
                beside = pltpu.roll(g, NY, 1)
                tile = jnp.where(lane < NY, pltpu.roll(outside, NY, 1), beside[:, :128])
                beside = jnp.concatenate([tile, beside[:, 128:]], axis=1)
            else:
                beside = pltpu.roll(g, cells - NY, 1)
                tile = jnp.where(lane >= 128 - NY, pltpu.roll(outside, 128 - NY, 1), beside[:, cells - 128 :])
                beside = jnp.concatenate([beside[:, : cells - 128], tile], axis=1)
            over = jnp.where(y_place == y_edge, 0.0, pltpu.roll(g, y_shift, 1))
            freq = jnp.sum(jnp.where(freq_lane == sub + i * NV1, freq_ref[...], 0.0), axis=1, keepdims=True)
            out_ref[here, :] = g - (speed_x * (g - beside) + speed * (g - over)) - freq * g
            return carry

        lax.fori_loop(0, rows // NV1, chunk, 0)

    @pl.when(rank >= NV1 // 2)
    def _():
        loop(1, 0)

    @pl.when(rank < NV1 // 2)
    def _():
        loop(cells - 1, NY - 1)


def base_part(positive, info, distribution, halo, pair_edge, frequency):
    rows, cells = distribution.shape
    part = rows // 2
    smem = pl.BlockSpec(memory_space=pltpu.SMEM)
    at = lambda i: (int(positive), 0)
    thin = pl.BlockSpec((part, 128), at)
    return pl.pallas_call(
        functools.partial(base_kernel, positive),
        grid=(1,),
        out_shape=jax.ShapeDtypeStruct((part, cells), jnp.float32),
        in_specs=[smem, pl.BlockSpec((part, cells), at), thin, thin, pl.BlockSpec((1, part), lambda i: (0, int(positive)))],
        out_specs=pl.BlockSpec((part, cells), lambda i: (0, 0)),
        compiler_params=pltpu.CompilerParams(vmem_limit_bytes=6 << 20),
        cost_estimate=pl.CostEstimate(flops=5_000_000, bytes_accessed=1_500_000, transcendentals=0),
    )(info, distribution, halo, pair_edge, frequency[None, :])


def per_device(distribution, kernel, frequency, accommodation, wall_class):
    rows, cells = distribution.shape
    ranks = lax.axis_size("vel")
    places = lax.axis_size("space")
    rank = lax.axis_index("vel")
    core = lax.axis_index("space") & 1
    f32, bf16 = jnp.float32, jnp.bfloat16
    half = ranks // 2

    ring = [(s * ranks + v, s * ranks + (v + (1 if s % 2 == 0 else -1)) % ranks) for s in range(places) for v in range(ranks)]
    pair = [(s, s ^ 1) for s in range(places)]
    beyond = [(s, (s + (1 if s % 2 else -1)) % places) for s in range(places)]

    cross = [
        (s * ranks + v, (s ^ 1) * ranks + (v + (-1 if s % 2 == 0 else 1)) % ranks) for s in range(places) for v in range(ranks)
    ]

    def hop(values, way=ring):
        return lax.ppermute(values, ("space", "vel"), way)

    def swap(values, way=pair):
        return lax.ppermute(values, "space", way)

    low = distribution.astype(bf16)
    held = [hop(low), hop(low, cross)]

    info = jnp.stack([rank, core])
    keep, share = wall_part(info, wall_class, accommodation, cells)
    keeps = [keep, swap(keep)]

    block = lax.broadcasted_iota(jnp.int32, (EXTRA, kernel.shape[1]), 1) // rows
    outgoing = (block < half) != (rank < half)
    weight = jnp.where(outgoing, jnp.abs(2 * block - (NV1 - 1)), 0).astype(bf16)
    wide = jnp.concatenate([kernel, weight], axis=0)

    def origin(step):
        return (rank + jnp.where(core == 0, -step, step)) & (ranks - 1)

    def part(step, values):
        return jnp.dot(
            lax.dynamic_slice_in_dim(wide, origin(step) * rows, rows, axis=1), values, preferred_element_type=f32
        )

    head, tail = low[:, :128], low[:, cells - 128 :]
    outer, inner = jnp.where(core == 0, head, tail), jnp.where(core == 0, tail, head)
    halo = swap(outer, beyond)
    pair_edge = swap(inner)
    base = []
    for positive in (False, True):
        base.append(base_part(positive, info, distribution, halo, pair_edge, frequency))

    sums = [part(0, low), None]
    due = [[], []]
    for step in range(1, half):
        for j in (0, 1):
            if step > 1:
                held[j] = hop(held[j])
                if step == ADD_AT and j == 0:
                    held[0], sums[0], base = lax.optimization_barrier((held[0], sums[0], base))
                elif step < half - 1:
                    held[j], sums[j] = lax.optimization_barrier((held[j], sums[j]))
        for j in (0, 1):
            mirrored = (jnp.where(origin(step) == ranks - 1 - rank, 1.0, 0.0), keeps[j], held[j])
            if step % 2 == 1 and (step > 1 or j == 0):
                due[j].append(mirrored)
            given = part(step, held[j])
            for flag, row, values in due[j]:
                given = given + jnp.pad(values.astype(f32) * flag * row, ((0, EXTRA), (0, 0)))
            due[j] = []
            if step == ADD_AT and j == 0:
                for i, piece in enumerate(base):
                    below = rows + EXTRA - (i + 1) * (rows // 2)
                    given = given + jnp.pad(piece, ((i * (rows // 2), below), (0, 0)))
            sums[j] = given if sums[j] is None else sums[j] + given
            if step == 1 and j == 1:
                due[j].append(mirrored)
    final = hop(held[0])
    given = swap(sums[1])

    acc = sums[0] + given
    return last_part(info, kernel, acc, final, share)


def solution(mesh):
    placed = (P("vel", "space"), P("vel", None), P("vel"), P(), P(None, "space"))
    return jax.shard_map(per_device, mesh=mesh, in_specs=placed, out_specs=P("vel", "space"), check_vma=False)
```

```python
import functools

import jax
import jax.numpy as jnp
import numpy as np
from jax import lax
from jax.experimental import pallas as pl
from jax.experimental.pallas import tpu as pltpu
from jax.sharding import PartitionSpec as P

NV1 = 16
NY = 32
SPACING = 9.6 / NV1
MIDDLE = (NV1 - 1) / 2.0
EXTRA = 16
ADD_AT = 6

courant_x = 0.05
courant_y = 0.15


POINTS = (np.arange(NV1) - MIDDLE) * SPACING
WEIGHTS = np.exp(-0.5 * POINTS * POINTS)
ZSUM = float(WEIGHTS.sum())
OUTFLOW = float((POINTS * WEIGHTS)[POINTS > 0].sum() / ZSUM)


def speed_y(rank):
    return courant_y * jnp.abs((rank.astype(jnp.float32) - MIDDLE) * SPACING)


def wall_kernel(info_ref, class_ref, alpha_ref, keep_ref, share_ref):
    cells = keep_ref.shape[1]
    rank = info_ref[0]
    side = jnp.where(rank < NV1 // 2, 1, 0)
    lane = lax.broadcasted_iota(jnp.int32, (1, cells), 1)
    alpha = jnp.zeros((1, cells), jnp.float32)
    for x in range(cells // NY):
        alpha = jnp.where(lane // NY == x, alpha_ref[class_ref[side, x]], alpha)
    at_wall = lane % NY == jnp.where(rank < NV1 // 2, NY - 1, 0)
    keep_ref[...] = jnp.where(at_wall, speed_y(rank) * (1.0 - alpha), 0.0)
    share_ref[...] = jnp.where(at_wall, alpha * (0.5 * SPACING / OUTFLOW), 0.0)


def wall_part(info, wall_class, accommodation, cells):
    smem = pl.BlockSpec(memory_space=pltpu.SMEM)
    vmem = pl.BlockSpec(memory_space=pltpu.VMEM)
    return pl.pallas_call(
        wall_kernel,
        out_shape=[jax.ShapeDtypeStruct((1, cells), jnp.float32)] * 2,
        in_specs=[smem, smem, smem],
        out_specs=[vmem, vmem],
        compiler_params=pltpu.CompilerParams(vmem_limit_bytes=1 << 20),
        cost_estimate=pl.CostEstimate(flops=100_000, bytes_accessed=10_000, transcendentals=0),
    )(info, wall_class, accommodation)


def last_kernel(info_ref, kernel_ref, acc_ref, far_ref, share_ref, out_ref):
    rows = out_ref.shape[0]
    rank = info_ref[0]
    far = (rank + NV1 // 2) & (NV1 - 1)
    values = far_ref[...]
    weight = jnp.abs(2 * far - (NV1 - 1)).astype(jnp.float32)
    flux = acc_ref[rows : rows + 1, :] + weight * jnp.sum(values.astype(jnp.float32), axis=0, keepdims=True)
    gain = jnp.dot(kernel_ref[...], values, preferred_element_type=jnp.float32)
    index = lax.broadcasted_iota(jnp.int32, (rows, 1), 0)
    vel_x = ((index // NV1).astype(jnp.float32) - MIDDLE) * SPACING
    vel_z = ((index % NV1).astype(jnp.float32) - MIDDLE) * SPACING
    vel_y = (rank.astype(jnp.float32) - MIDDLE) * SPACING
    maxwell = jnp.exp(-0.5 * (vel_x * vel_x + vel_y * vel_y + vel_z * vel_z)) * (speed_y(rank) / ZSUM**3)
    out_ref[...] = acc_ref[:rows, :] + gain + maxwell * (flux * share_ref[...])


def last_part(info, kernel, acc, far, share):
    rows, cells = far.shape
    width = cells
    far_of = lambda info: (info[0] + NV1 // 2) & (NV1 - 1)
    return pl.pallas_call(
        last_kernel,
        grid_spec=pltpu.PrefetchScalarGridSpec(
            num_scalar_prefetch=1,
            grid=(1,),
            in_specs=[
                pl.BlockSpec((rows, rows), lambda i, info: (0, far_of(info))),
                pl.BlockSpec((acc.shape[0], width), lambda i, info: (0, i)),
                pl.BlockSpec((rows, width), lambda i, info: (0, i)),
                pl.BlockSpec((1, width), lambda i, info: (0, i)),
            ],
            out_specs=pl.BlockSpec((rows, width), lambda i, info: (0, i)),
        ),
        out_shape=jax.ShapeDtypeStruct((rows, cells), jnp.float32),
        compiler_params=pltpu.CompilerParams(vmem_limit_bytes=10 << 20),
        cost_estimate=pl.CostEstimate(flops=2 * rows * rows * cells, bytes_accessed=3_000_000, transcendentals=0),
    )(info, kernel, acc, far, share)


def base_kernel(positive, info_ref, d_ref, halo_ref, pair_ref, freq_ref, out_ref):
    rows, cells = d_ref.shape
    rank = info_ref[0]
    core = info_ref[1]
    speed = speed_y(rank)
    sub = lax.broadcasted_iota(jnp.int32, (NV1, rows), 0)
    freq_lane = lax.broadcasted_iota(jnp.int32, (NV1, rows), 1)
    y_place = lax.broadcasted_iota(jnp.int32, (NV1, cells), 1) % NY
    lane = lax.broadcasted_iota(jnp.int32, (NV1, 128), 1)
    from_pair = core if positive else 1 - core

    def loop(y_shift, y_edge):
        def chunk(i, carry):
            here = pl.ds(pl.multiple_of(i * NV1, NV1), NV1)
            index_x = i + (rows // NV1 if positive else 0)
            speed_x = courant_x * jnp.abs((index_x.astype(jnp.float32) - MIDDLE) * SPACING)
            g = d_ref[here, :]
            outside = jnp.where(from_pair == 1, pair_ref[here, :], halo_ref[here, :]).astype(jnp.float32)
            if positive:
                beside = pltpu.roll(g, NY, 1)
                tile = jnp.where(lane < NY, pltpu.roll(outside, NY, 1), beside[:, :128])
                beside = jnp.concatenate([tile, beside[:, 128:]], axis=1)
            else:
                beside = pltpu.roll(g, cells - NY, 1)
                tile = jnp.where(lane >= 128 - NY, pltpu.roll(outside, 128 - NY, 1), beside[:, cells - 128 :])
                beside = jnp.concatenate([beside[:, : cells - 128], tile], axis=1)
            over = jnp.where(y_place == y_edge, 0.0, pltpu.roll(g, y_shift, 1))
            freq = jnp.sum(jnp.where(freq_lane == sub + i * NV1, freq_ref[...], 0.0), axis=1, keepdims=True)
            out_ref[here, :] = g - (speed_x * (g - beside) + speed * (g - over)) - freq * g
            return carry

        lax.fori_loop(0, rows // NV1, chunk, 0)

    @pl.when(rank >= NV1 // 2)
    def _():
        loop(1, 0)

    @pl.when(rank < NV1 // 2)
    def _():
        loop(cells - 1, NY - 1)


def base_part(positive, info, distribution, halo, pair_edge, frequency):
    rows, cells = distribution.shape
    part = rows // 2
    smem = pl.BlockSpec(memory_space=pltpu.SMEM)
    at = lambda i: (int(positive), 0)
    thin = pl.BlockSpec((part, 128), at)
    return pl.pallas_call(
        functools.partial(base_kernel, positive),
        grid=(1,),
        out_shape=jax.ShapeDtypeStruct((part, cells), jnp.float32),
        in_specs=[smem, pl.BlockSpec((part, cells), at), thin, thin, pl.BlockSpec((1, part), lambda i: (0, int(positive)))],
        out_specs=pl.BlockSpec((part, cells), lambda i: (0, 0)),
        compiler_params=pltpu.CompilerParams(vmem_limit_bytes=6 << 20),
        cost_estimate=pl.CostEstimate(flops=5_000_000, bytes_accessed=1_500_000, transcendentals=0),
    )(info, distribution, halo, pair_edge, frequency[None, :])


def per_device(distribution, kernel, frequency, accommodation, wall_class):
    rows, cells = distribution.shape
    ranks = lax.axis_size("vel")
    places = lax.axis_size("space")
    rank = lax.axis_index("vel")
    core = lax.axis_index("space") & 1
    f32, bf16 = jnp.float32, jnp.bfloat16
    half = ranks // 2

    ring = [(s * ranks + v, s * ranks + (v + (1 if s % 2 == 0 else -1)) % ranks) for s in range(places) for v in range(ranks)]
    pair = [(s, s ^ 1) for s in range(places)]
    beyond = [(s, (s + (1 if s % 2 else -1)) % places) for s in range(places)]

    cross = [
        (s * ranks + v, (s ^ 1) * ranks + (v + (-1 if s % 2 == 0 else 1)) % ranks) for s in range(places) for v in range(ranks)
    ]

    def hop(values, way=ring):
        return lax.ppermute(values, ("space", "vel"), way)

    def swap(values, way=pair):
        return lax.ppermute(values, "space", way)

    low = distribution.astype(bf16)
    held = [hop(low), hop(low, cross)]

    info = jnp.stack([rank, core])
    keep, share = wall_part(info, wall_class, accommodation, cells)
    keeps = [keep, swap(keep)]

    block = lax.broadcasted_iota(jnp.int32, (EXTRA, kernel.shape[1]), 1) // rows
    outgoing = (block < half) != (rank < half)
    weight = jnp.where(outgoing, jnp.abs(2 * block - (NV1 - 1)), 0).astype(bf16)
    wide = jnp.concatenate([kernel, weight], axis=0)

    def origin(step):
        return (rank + jnp.where(core == 0, -step, step)) & (ranks - 1)

    def part(step, values):
        return jnp.dot(
            lax.dynamic_slice_in_dim(wide, origin(step) * rows, rows, axis=1), values, preferred_element_type=f32
        )

    head, tail = low[:, :128], low[:, cells - 128 :]
    outer, inner = jnp.where(core == 0, head, tail), jnp.where(core == 0, tail, head)
    halo = swap(outer, beyond)
    pair_edge = swap(inner)
    base = []
    for positive in (False, True):
        base.append(base_part(positive, info, distribution, halo, pair_edge, frequency))

    sums = [part(0, low), None]
    due = [[], []]
    for step in range(1, half):
        for j in (0, 1):
            if step > 1:
                held[j] = hop(held[j])
                if step == ADD_AT and j == 0:
                    held[0], sums[0], base = lax.optimization_barrier((held[0], sums[0], base))
                elif step < half - 1:
                    held[j], sums[j] = lax.optimization_barrier((held[j], sums[j]))
        for j in (0, 1):
            mirrored = (jnp.where(origin(step) == ranks - 1 - rank, 1.0, 0.0), keeps[j], held[j])
            if step % 2 == 1 and (step > 1 or j == 0):
                due[j].append(mirrored)
            given = part(step, held[j])
            for flag, row, values in due[j]:
                given = given + jnp.pad(values.astype(f32) * flag * row, ((0, EXTRA), (0, 0)))
            due[j] = []
            if step == ADD_AT and j == 0:
                for i, piece in enumerate(base):
                    below = rows + EXTRA - (i + 1) * (rows // 2)
                    given = given + jnp.pad(piece, ((i * (rows // 2), below), (0, 0)))
            sums[j] = given if sums[j] is None else sums[j] + given
            if step == 1 and j == 1:
                due[j].append(mirrored)
    final = hop(held[0])
    given = swap(sums[1])

    acc = sums[0] + given
    return last_part(info, kernel, acc, final, share)


def solution(mesh):
    placed = (P("vel", "space"), P("vel", None), P("vel"), P(), P(None, "space"))
    return jax.shard_map(per_device, mesh=mesh, in_specs=placed, out_specs=P("vel", "space"), check_vma=False)
```
